32 devices in a mesh: grp: 4 (over x, core), own: 8 (over z, y).
Axes of the slice: x: 2, y: 2, z: 4, core: 2. Of those that a mesh axis runs over, the one named last changes fastest.
Arguments:
- orbitals: bfloat16 [32, 32, 1024], P(('grp', 'own')), may hold values from -3 to 3
- offsets: int32 [32, 2], P(('grp', 'own')), may hold values from 0 to 32
- pairs: int32 [32, 2], P('grp'), may hold values from 0 to 7, as said below
- ext_pot: bfloat16 [32, 4096], replicated, may hold values from -6 to 6
Outputs:
- gradient: float32 [32, 32, 1024], P(('grp', 'own'))
The draws below stay inside these ranges and needn't reach their ends.
Inputs may be any that keep to these rules, and one draw needn't show every extreme that they name: `pairs`: rows g * 8 to g * 8 + 7 belong to group g; each row names two different orbitals of the group. Calling owner o the device holding orbital o of a group, at most 2 rows of a group have orbital o as their first orbital, and in every group some owner has exactly 2.
All inputs are finite; a program needn't handle non-finite values.
Results may differ from the reference program's by a relative error of at most 0.0006.
Values may be sent and summed in bfloat16 or wider, within the bound.
A program may use at most 64 MiB of HBM per device.

```python
import math
import jax
import jax.numpy as jnp
from jax import lax

B = 32
BZ = 32
G = 64
ORB_DEV = 1
TASK_CAP = 2
GROUPS = 4
OWNERS = 8
ORB_GRP = 8
ORBITALS = 32
PAIRS_GRP = 8
PAIRS = 32


def draw_pairs(key, part):

    def one_group(group):
        base = jax.random.fold_in(jax.random.fold_in(key, 7001), group)
        keys = jax.random.split(base, 5)
        heavy = jax.random.randint(keys[0], (), 0, OWNERS)
        spare = jax.random.permutation(keys[1], (OWNERS - 1) * TASK_CAP)[:PAIRS_GRP - TASK_CAP]
        others = (spare // TASK_CAP).astype(jnp.int32)
        others = others + (others >= heavy).astype(jnp.int32)
        owners = jnp.concatenate([jnp.full((TASK_CAP,), heavy, jnp.int32), others])
        first = owners * ORB_DEV + jax.random.randint(keys[2], (PAIRS_GRP,), 0, ORB_DEV)
        second = (first + jax.random.randint(keys[3], (PAIRS_GRP,), 1, ORB_GRP)) % ORB_GRP
        listed = jnp.stack([first, second], axis=1)
        ranking = jax.random.permutation(keys[4], PAIRS_GRP)
        return listed[ranking]
    every = jax.vmap(one_group)(jnp.arange(GROUPS, dtype=jnp.int32))
    return every.reshape(PAIRS, 2).astype(jnp.int32)


def set_ends(drawn, stream_key, least, largest):
    longest = drawn.shape.index(max(drawn.shape))
    spots = []
    for shift in (0, 1):
        where = [jax.random.randint(jax.random.fold_in(stream_key, axis), (), 0, length) for axis, length in enumerate(drawn.shape)]
        where[longest] = (where[longest] + shift) % drawn.shape[longest]
        spots.append(tuple(where))
    return drawn.at[spots[0]].set(least).at[spots[1]].set(largest)


def block_scale(key, dims, shards, least, high):
    level, own = 1.0, jax.random.fold_in(key, 6)
    for position, blocks in shards:
        draws = jnp.exp(jax.random.uniform(jax.random.fold_in(own, position), (blocks,), jnp.float32, least / len(shards), high / len(shards)))
        level = level * jnp.repeat(draws, dims[position] // blocks).reshape([-1 if axis == position else 1 for axis in range(len(dims))])
    return level


def scatter_about(own_key, dims, scale, limit, cuts=(), kind=jnp.bfloat16):
    entries = jax.random.normal(own_key, dims, jnp.float32) * scale
    if len(cuts) > 0:
        entries = block_scale(own_key, dims, cuts, -0.22, 0.18) * entries
    return jnp.clip(entries, min=-limit, max=limit).astype(kind)


def setup_inputs(seed: int = 0) -> dict:
    splits = jax.random.split(jax.random.key(seed), 5)
    return {
        "orbitals": scatter_about(splits[0], (ORBITALS, BZ, B * B), 0.5, 3.0, ((0, 32),)),
        "offsets": set_ends(jax.random.randint(splits[1], (ORBITALS, 2), 0, G - B + 1), jax.random.fold_in(splits[1], 1), 0, G - B).astype(jnp.int32),
        "pairs": draw_pairs(jax.random.fold_in(splits[4], 71), 0),
        "ext_pot": scatter_about(splits[3], (BZ, G * G), 1.0, 6.0),
    }


SCREEN = 0.0025
MIXING = 0.25
EXCHANGE_COEF = (3.0 / math.pi) ** (1.0 / 3.0)


def wave_squares(length):
    positions = jnp.arange(length, dtype=jnp.int32)
    signed = jnp.where(positions < length // 2, positions, positions - length)
    wavenumber = (2.0 * math.pi / length) * signed.astype(jnp.float32)
    return wavenumber * wavenumber


def green_table(depth, width):
    along_z = wave_squares(2 * depth)
    along_y = wave_squares(2 * width)
    squared_sum = along_z[:, None, None] + along_y[None, :, None] + along_y[None, None, :]
    return (4.0 * math.pi) / (squared_sum + SCREEN)


def shifted(box_data, shift_y, shift_x):
    padded = jnp.pad(box_data, ((0, 0), (B, B), (B, B)))
    anchor = jnp.zeros((), jnp.int32)
    corner = (anchor, (B + shift_y).astype(jnp.int32), (B + shift_x).astype(jnp.int32))
    return lax.dynamic_slice(padded, corner, (BZ, B, B))


def poisson_solve(pair_density, green_values):
    padded = jnp.pad(pair_density, ((0, BZ), (0, B), (0, B)))
    spectrum = jnp.fft.fftn(padded) * green_values
    return jnp.real(jnp.fft.ifftn(spectrum))[:BZ, :B, :B]


def reference(orbitals, offsets, pairs, ext_pot):
    box_data = orbitals.astype(jnp.float32).reshape(ORBITALS, BZ, B, B)
    green_values = green_table(BZ, B)

    def add_pair(item, running):
        group = (item // PAIRS_GRP).astype(jnp.int32)
        first = (pairs[item, 0] + group * ORB_GRP).astype(jnp.int32)
        second = (pairs[item, 1] + group * ORB_GRP).astype(jnp.int32)
        shift = offsets[second] - offsets[first]
        near_box = box_data[first]
        moved_box = shifted(box_data[second], -shift[0], -shift[1])
        potential_box = poisson_solve(near_box * moved_box, green_values)
        running = running.at[first].add(potential_box * moved_box)
        return running.at[second].add(shifted(potential_box * near_box, shift[0], shift[1]))

    exchange = lax.fori_loop(0, PAIRS, add_pair, jnp.zeros((ORBITALS, BZ, B, B), jnp.float32))

    def add_box(item, density):
        anchor = jnp.zeros((), jnp.int32)
        corner = (anchor, offsets[item, 0].astype(jnp.int32), offsets[item, 1].astype(jnp.int32))
        current = lax.dynamic_slice(density, corner, (BZ, B, B))
        values = box_data[item]
        return lax.dynamic_update_slice(density, current + values * values, corner)

    density = lax.fori_loop(0, ORBITALS, add_box, jnp.zeros((BZ, G, G), jnp.float32))
    potential = ext_pot.astype(jnp.float32).reshape(BZ, G, G) - EXCHANGE_COEF * jnp.cbrt(density)

    def read_box(item):
        anchor = jnp.zeros((), jnp.int32)
        corner = (anchor, offsets[item, 0].astype(jnp.int32), offsets[item, 1].astype(jnp.int32))
        return lax.dynamic_slice(potential, corner, (BZ, B, B))

    local_potential = lax.map(read_box, jnp.arange(ORBITALS, dtype=jnp.int32))
    gradient = local_potential * box_data - MIXING * exchange
    return gradient.reshape(ORBITALS, BZ, B * B)
```

```python
import functools
import math

import jax
import jax.numpy as jnp
from jax import lax
from jax.experimental import pallas as pl
from jax.experimental.pallas import tpu as pltpu
from jax.sharding import PartitionSpec as P

SCREEN = 0.0025
MIXING = 0.25
EXCHANGE_COEF = (3.0 / math.pi) ** (1.0 / 3.0)
PRECISE = lax.Precision.HIGHEST
VMEM = pltpu.VMEM


def side_of(cells):
    return math.isqrt(cells)


def cas_table(length, count):
    row = lax.broadcasted_iota(jnp.int32, (length, count), 0)
    col = lax.broadcasted_iota(jnp.int32, (length, count), 1)
    angle = 2.0 * math.pi / length * (row * col % length).astype(jnp.float32)
    return jnp.cos(angle) + jnp.sin(angle)


def wave_squares(length):
    positions = jnp.arange(length, dtype=jnp.int32)
    signed = jnp.where(positions < length // 2, positions, positions - length)
    wavenumber = 2.0 * math.pi / length * signed.astype(jnp.float32)
    return wavenumber * wavenumber


def green_table(depth, width):
    along_z = wave_squares(2 * depth)
    along_y = wave_squares(2 * width)
    squared_sum = along_z[:, None, None] + along_y[None, :, None] + along_y[None, None, :]
    return 4.0 * math.pi / (squared_sum + SCREEN)


def rotate(pattern, matrix, operand):
    return jnp.einsum(pattern, matrix, operand, precision=PRECISE, preferred_element_type=jnp.float32)


def poisson_solve(density, transforms):
    green_values, along_z, along_y = transforms
    value = rotate("kz,zyx->kyx", along_z, density)
    value = rotate("ky,zyx->zkx", along_y, value)
    value = rotate("kx,zyx->zyk", along_y, value)
    value = value * green_values
    value = rotate("kx,zyk->zyx", along_y, value)
    value = rotate("ky,zkx->zyx", along_y, value)
    return rotate("kz,kyx->zyx", along_z, value)


def shifted(box_data, shift_y, shift_x):
    depth, side, _ = box_data.shape
    padded = jnp.pad(box_data, ((0, 0), (side, side), (side, side)))
    anchor = jnp.zeros((), jnp.int32)
    corner = (anchor, (side + shift_y).astype(jnp.int32), (side + shift_x).astype(jnp.int32))
    return lax.dynamic_slice(padded, corner, (depth, side, side))


def placer(starts, row_count, side):
    grid_index = lax.broadcasted_iota(jnp.int32, (starts.shape[0], row_count, side), 1)
    cell_index = lax.broadcasted_iota(jnp.int32, (starts.shape[0], row_count, side), 2)
    return (grid_index == cell_index + starts[:, None, None]).astype(jnp.float32)


def greet(axis, count):
    me = lax.axis_index(axis)
    barrier = pltpu.get_barrier_semaphore()

    def hello(step, carry):
        peer = lax.rem(me + step, count)
        pl.semaphore_signal(barrier, inc=1, device_id={axis: peer}, device_id_type=pl.DeviceIdType.MESH)
        return carry

    lax.fori_loop(1, count, hello, 0)
    pl.semaphore_wait(barrier, count - 1)


def gather_kernel(axis, count, *refs):
    pieces = (len(refs) - 3) // 2
    sources, targets = refs[:pieces], refs[pieces : 2 * pieces]
    send_sem, recv_sem, local_sem = refs[2 * pieces :]
    me = lax.axis_index(axis)
    greet(axis, count)

    def copy_to(piece, step):
        return pltpu.make_async_remote_copy(
            src_ref=sources[piece],
            dst_ref=targets[piece].at[me],
            send_sem=send_sem.at[piece, step],
            recv_sem=recv_sem.at[piece, step],
            device_id={axis: lax.rem(me + step, count)},
            device_id_type=pl.DeviceIdType.MESH,
        )

    for step in range(1, count):
        for piece in range(pieces):
            copy_to(piece, step).start()
    for piece in range(pieces):
        own = pltpu.make_async_copy(sources[piece], targets[piece].at[me], local_sem.at[piece])
        own.start()
        own.wait()
    for step in range(1, count):
        for piece in range(pieces):
            copy_to(piece, step).wait()


def gather(axis, count, collective_id, *arrays):
    pieces = len(arrays)
    return pl.pallas_call(
        functools.partial(gather_kernel, axis, count),
        out_shape=[jax.ShapeDtypeStruct((count,) + a.shape, a.dtype) for a in arrays],
        in_specs=[pl.BlockSpec(memory_space=VMEM)] * pieces,
        out_specs=[pl.BlockSpec(memory_space=VMEM)] * pieces,
        scratch_shapes=[
            pltpu.SemaphoreType.DMA((pieces, count)),
            pltpu.SemaphoreType.DMA((pieces, count)),
            pltpu.SemaphoreType.DMA((pieces,)),
        ],
        compiler_params=pltpu.CompilerParams(collective_id=collective_id, has_side_effects=True),
        name="gather_" + axis,
    )(*arrays)


def return_kernel(axis, count, terms, read, phi, out, term_slots, read_slots, send_sem, recv_sem):
    me = lax.axis_index(axis)
    depth = read.shape[1]
    greet(axis, count)

    def copies(step):
        peer = lax.rem(me + step, count)
        pair = []
        for piece, (source, slots) in enumerate(((terms, term_slots), (read, read_slots))):
            pair.append(
                pltpu.make_async_remote_copy(
                    src_ref=source.at[peer],
                    dst_ref=slots.at[me],
                    send_sem=send_sem.at[piece, step],
                    recv_sem=recv_sem.at[piece, step],
                    device_id={axis: peer},
                    device_id_type=pl.DeviceIdType.MESH,
                )
            )
        return pair

    for step in range(1, count):
        for copy in copies(step):
            copy.start()
    total = terms[me]
    for step in range(1, count):
        for copy in copies(step):
            copy.wait()
        total = total + term_slots[lax.rem(me + count - step, count)]
    read_slots[me] = read[me]
    for owner in range(count):
        rows = slice(owner * depth, (owner + 1) * depth)
        out[rows, :] = read_slots[owner] * phi[rows, :] - MIXING * total[rows, :]


def send_back(axis, count, collective_id, terms, read, phi):
    return pl.pallas_call(
        functools.partial(return_kernel, axis, count),
        out_shape=jax.ShapeDtypeStruct(phi.shape, jnp.float32),
        in_specs=[pl.BlockSpec(memory_space=VMEM)] * 3,
        out_specs=pl.BlockSpec(memory_space=VMEM),
        scratch_shapes=[
            VMEM(terms.shape, jnp.float32),
            VMEM(read.shape, jnp.float32),
            pltpu.SemaphoreType.DMA((2, count)),
            pltpu.SemaphoreType.DMA((2, count)),
        ],
        compiler_params=pltpu.CompilerParams(collective_id=collective_id, has_side_effects=True),
        name="send_back",
    )(terms, read, phi)


def body(owners, groups, orbitals, offsets, pairs, ext_pot):
    owner = lax.axis_index("own")
    _, levels, cells = orbitals.shape
    side = side_of(cells)
    grid = side_of(ext_pot.shape[1])
    depth = levels // owners
    padded = jnp.pad(offsets, ((0, 7), (0, 126)))
    boxes, spread = gather("own", owners, 0, orbitals[0], padded)
    corners = spread[:, 0, :2]

    planes = lax.dynamic_slice_in_dim(boxes, owner * depth, depth, 1).astype(jnp.float32)
    planes = planes.reshape(owners, depth, side, side)
    along_rows = placer(corners[:, 0], grid, side)
    along_cols = placer(corners[:, 1], grid, side)
    partial = jnp.einsum("izyx,ihx->izyh", planes * planes, along_cols, precision=PRECISE)
    partial = jnp.einsum("igy,izyh->zgh", along_rows, partial, precision=PRECISE)
    (shares,) = gather("grp", groups, 1, partial.reshape(depth, grid * grid))
    density = jnp.sum(shares, axis=0)
    external = lax.dynamic_slice_in_dim(ext_pot, owner * depth, depth, 0)
    potential = external.astype(jnp.float32) - EXCHANGE_COEF * jnp.cbrt(density)
    potential = potential.reshape(depth, grid, grid)
    read = jnp.einsum("igy,zgh->izyh", along_rows, potential, precision=PRECISE)
    read = jnp.einsum("izyh,ihx->izyx", read, along_cols, precision=PRECISE)
    read = read.reshape(owners, depth, cells)

    transforms = (
        green_table(levels, side) * (1.0 / float(8 * levels * cells)),
        cas_table(2 * levels, levels),
        cas_table(2 * side, side),
    )
    terms = jnp.zeros((owners, levels, cells), jnp.float32)
    each = pairs.shape[0] // owners
    slots = jnp.arange(owners, dtype=jnp.int32)
    for turn in range(each):
        first = pairs[owner * each + turn, 0]
        second = pairs[owner * each + turn, 1]
        shift = corners[second] - corners[first]
        near = boxes[first].astype(jnp.float32).reshape(levels, side, side)
        far = boxes[second].astype(jnp.float32).reshape(levels, side, side)
        moved = shifted(far, -shift[0], -shift[1])
        field = poisson_solve(near * moved, transforms)
        to_first = (field * moved).reshape(levels, cells)
        to_second = shifted(field * near, shift[0], shift[1]).reshape(levels, cells)
        terms = terms + jnp.where((slots == first)[:, None, None], to_first, 0.0)
        terms = terms + jnp.where((slots == second)[:, None, None], to_second, 0.0)
    gradient = send_back("own", owners, 2, terms, read, orbitals[0].astype(jnp.float32))
    return gradient[None]


def solution(mesh):
    in_specs = (P(("grp", "own"), None, None), P(("grp", "own"), None), P("grp", None), P())
    out_specs = P(("grp", "own"), None, None)
    run = functools.partial(body, mesh.shape["own"], mesh.shape["grp"])
    return jax.shard_map(run, mesh=mesh, in_specs=in_specs, out_specs=out_specs, check_vma=False)
```

```python
import functools
import math

import jax
import jax.numpy as jnp
from jax import lax
from jax.experimental import pallas as pl
from jax.experimental.pallas import tpu as pltpu
from jax.sharding import PartitionSpec as P

SCREEN = 0.0025
MIXING = 0.25
EXCHANGE_COEF = (3.0 / math.pi) ** (1.0 / 3.0)
PRECISE = lax.Precision.HIGHEST
VMEM = pltpu.VMEM


def side_of(cells):
    return math.isqrt(cells)


def cas_table(length, count):
    row = lax.broadcasted_iota(jnp.int32, (length, count), 0)
    col = lax.broadcasted_iota(jnp.int32, (length, count), 1)
    angle = 2.0 * math.pi / length * (row * col % length).astype(jnp.float32)
    return jnp.cos(angle) + jnp.sin(angle)


def wave_squares(length):
    positions = jnp.arange(length, dtype=jnp.int32)
    signed = jnp.where(positions < length // 2, positions, positions - length)
    wavenumber = 2.0 * math.pi / length * signed.astype(jnp.float32)
    return wavenumber * wavenumber


def green_table(depth, width):
    along_z = wave_squares(2 * depth)
    along_y = wave_squares(2 * width)
    squared_sum = along_z[:, None, None] + along_y[None, :, None] + along_y[None, None, :]
    return 4.0 * math.pi / (squared_sum + SCREEN)


def rotate(pattern, matrix, operand):
    return jnp.einsum(pattern, matrix, operand, precision=PRECISE, preferred_element_type=jnp.float32)


def placer(starts, row_count, side):
    grid_index = lax.broadcasted_iota(jnp.int32, (starts.shape[0], row_count, side), 1)
    cell_index = lax.broadcasted_iota(jnp.int32, (starts.shape[0], row_count, side), 2)
    return (grid_index == cell_index + starts[:, None, None]).astype(jnp.float32)


def plane_split(count):
    rows = 1 << ((count.bit_length() - 1) // 2)
    return count // rows, rows


def relay_kernel(count, pieces, exchanged, *refs):
    far, near = plane_split(count)
    sources, slabs = refs[:pieces], refs[pieces : pieces + exchanged]
    refs = refs[pieces + exchanged :]
    targets, landings = refs[:pieces], refs[pieces : pieces + exchanged]
    send_sem, recv_sem, local_sem, slab_send, slab_recv = refs[pieces + exchanged :]
    me = lax.axis_index("own")
    z = me // near
    y = lax.rem(me, near)
    barrier = pltpu.get_barrier_semaphore()

    def across(step):
        return z * near + lax.rem(y + step, near)

    def signal(peer):
        pl.semaphore_signal(barrier, inc=1, device_id={"own": peer}, device_id_type=pl.DeviceIdType.MESH)

    if exchanged:
        for step in range(1, count):
            signal(lax.rem(me + step, count))
        pl.semaphore_wait(barrier, count - 1)
    else:
        for step in range(1, near):
            signal(across(step))
        pl.when(z > 0)(lambda: signal(me - near))
        pl.when(z < far - 1)(lambda: signal(me + near))
        pl.semaphore_wait(barrier, near - 1 + (z > 0).astype(jnp.int32) + (z < far - 1).astype(jnp.int32))

    parts = []
    for piece, source in enumerate(sources):
        rows = source.shape[0]
        if piece == 0:
            parts.append((piece, 0, rows // 2, False))
            parts.append((piece, rows // 2, rows // 2, True))
        else:
            parts.append((piece, 0, rows, True))
    fronts = [i for i, part in enumerate(parts) if not part[3]]
    backs = [i for i, part in enumerate(parts) if part[3]]

    def copy(index, origin, lane, peer, own):
        piece, start, size, _ = parts[index]
        rows = pl.ds(start, size)
        source = sources[piece].at[rows] if own else targets[piece].at[origin, rows]
        return pltpu.make_async_remote_copy(
            src_ref=source,
            dst_ref=targets[piece].at[origin, rows],
            send_sem=send_sem.at[index, origin, lane],
            recv_sem=recv_sem.at[index, origin],
            device_id={"own": peer},
            device_id_type=pl.DeviceIdType.MESH,
        )

    def slab_copy(index, step):
        peer = lax.rem(me + step, count)
        return pltpu.make_async_remote_copy(
            src_ref=slabs[index].at[peer],
            dst_ref=landings[index].at[me],
            send_sem=slab_send.at[index, step],
            recv_sem=slab_recv.at[index, step],
            device_id={"own": peer},
            device_id_type=pl.DeviceIdType.MESH,
        )

    def both(index, origin, own, act):
        pl.when(z < far - 1)(lambda: act(copy(index, origin, 0, me + near, own)))
        pl.when(z > 0)(lambda: act(copy(index, origin, 1, me - near, own)))

    def sideways(index, origin, own, act):
        for step in range(1, near):
            act(copy(index, origin, 1 + step, across(step), own))

    def start(item):
        item.start()

    def sent(item):
        item.wait_send()

    def arrived(index, origin):
        copy(index, origin, 0, me, False).wait_recv()

    for index in backs:
        both(index, me, True, start)
    for index in fronts:
        sideways(index, me, True, start)
    for index in backs:
        sideways(index, me, True, start)
    for index in range(exchanged):
        for step in range(1, count):
            slab_copy(index, step).start()
    for index in fronts:
        both(index, me, True, start)
    locals_ = [
        pltpu.make_async_copy(sources[piece], targets[piece].at[me], local_sem.at[piece]) for piece in range(pieces)
    ]
    for index in range(exchanged):
        locals_.append(pltpu.make_async_copy(slabs[index].at[me], landings[index].at[me], local_sem.at[pieces + index]))
    for item in locals_:
        item.start()
    for step in range(1, near):
        for index in fronts:
            arrived(index, across(step))
            both(index, across(step), False, start)

    def hop(distance, direction):
        here = z - direction * distance
        inside = (here >= 0) & (here < far)
        onward = inside & (z + direction >= 0) & (z + direction < far)
        lane = 0 if direction > 0 else 1
        neighbour = me + direction * near
        return here, inside, onward, lane, neighbour

    def travel(act, receive):
        for distance in range(1, far):
            for direction in (1, -1):
                here, inside, onward, lane, neighbour = hop(distance, direction)
                for index in backs:
                    origin = here * near + y
                    if receive:
                        pl.when(inside)(functools.partial(arrived, index, origin))
                    pl.when(onward)(lambda: act(copy(index, origin, lane, neighbour, False)))
                    pl.when(inside)(lambda: sideways(index, origin, False, act))
                for index in fronts:
                    for step in range(near):
                        origin = here * near + lax.rem(y + step, near)
                        if receive:
                            pl.when(inside)(functools.partial(arrived, index, origin))
                        pl.when(onward)(lambda: act(copy(index, origin, lane, neighbour, False)))

    travel(start, True)
    for level in range(far):
        for step in range(1, near):
            for index in backs:
                arrived(index, level * near + lax.rem(y + step, near))
    for index in range(exchanged):
        for step in range(1, count):
            slab_copy(index, step).wait()
    for index in backs + fronts:
        both(index, me, True, sent)
        sideways(index, me, True, sent)
    for step in range(1, near):
        for index in fronts:
            both(index, across(step), False, sent)
    travel(sent, False)
    for item in locals_:
        item.wait()


def relay(count, collective_id, arrays, slabs=()):
    pieces, exchanged = len(arrays), len(slabs)
    _, near = plane_split(count)
    shapes = [jax.ShapeDtypeStruct((count,) + a.shape, a.dtype) for a in arrays]
    shapes += [jax.ShapeDtypeStruct(a.shape, a.dtype) for a in slabs]
    return pl.pallas_call(
        functools.partial(relay_kernel, count, pieces, exchanged),
        out_shape=shapes,
        in_specs=[pl.BlockSpec(memory_space=VMEM)] * (pieces + exchanged),
        out_specs=[pl.BlockSpec(memory_space=VMEM)] * (pieces + exchanged),
        scratch_shapes=[
            pltpu.SemaphoreType.DMA((pieces + 1, count, near + 1)),
            pltpu.SemaphoreType.DMA((pieces + 1, count)),
            pltpu.SemaphoreType.DMA((pieces + exchanged,)),
            pltpu.SemaphoreType.DMA((max(exchanged, 1), count)),
            pltpu.SemaphoreType.DMA((max(exchanged, 1), count)),
        ],
        compiler_params=pltpu.CompilerParams(collective_id=collective_id, has_side_effects=True),
        name="relay",
    )(*arrays, *slabs)


def slide(value, shift_y, shift_x, side):
    cells = value.shape[1]
    lane = lax.broadcasted_iota(jnp.int32, value.shape, 1)
    y = lane // side - shift_y
    x = lax.rem(lane, side) - shift_x
    inside = (y >= 0) & (y < side) & (x >= 0) & (x < side)
    amount = lax.rem(shift_y * side + shift_x + 2 * cells, cells)
    return jnp.where(inside, pltpu.roll(value, amount, axis=1), 0.0)


def pair_kernel(each, side, owner_ref, pairs, corners, boxes, rho):
    base = owner_ref[0] * each
    for turn in range(each):
        first, second = pairs[base + turn, 0], pairs[base + turn, 1]
        dy = corners[second, 0] - corners[first, 0]
        dx = corners[second, 1] - corners[first, 1]
        moved = slide(boxes[second].astype(jnp.float32), dy, dx, side)
        rho[turn] = boxes[first].astype(jnp.float32) * moved


def combine_kernel(side, owner_ref, pairs, corners, boxes, fields, read, phi, out):
    me = owner_ref[0]
    owners, depth, _ = read.shape
    own = phi[...].astype(jnp.float32)
    for owner in range(owners):
        rows = slice(owner * depth, (owner + 1) * depth)
        out[rows, :] = read[owner] * own[rows, :]

    def step(row, carry):
        first, second = pairs[row, 0], pairs[row, 1]
        dy = corners[second, 0] - corners[first, 0]
        dx = corners[second, 1] - corners[first, 1]

        @pl.when(first == me)
        def _():
            moved = slide(boxes[second].astype(jnp.float32), dy, dx, side)
            out[...] -= MIXING * fields[row] * moved

        @pl.when(second == me)
        def _():
            product = fields[row] * boxes[first].astype(jnp.float32)
            out[...] -= MIXING * slide(product, -dy, -dx, side)

        return carry

    lax.fori_loop(0, pairs.shape[0], step, 0)


def local_call(kernel, shape, scalars, arrays, name):
    return pl.pallas_call(
        kernel,
        out_shape=jax.ShapeDtypeStruct(shape, jnp.float32),
        in_specs=[pl.BlockSpec(memory_space=pltpu.SMEM)] * len(scalars)
        + [pl.BlockSpec(memory_space=VMEM)] * len(arrays),
        out_specs=pl.BlockSpec(memory_space=VMEM),
        name=name,
    )(*scalars, *arrays)


def body(owners, groups, orbitals, offsets, pairs, ext_pot):
    owner = lax.axis_index("own")
    _, levels, cells = orbitals.shape
    side = side_of(cells)
    grid = side_of(ext_pot.shape[1])
    depth = levels // owners
    padded = jnp.pad(offsets, ((0, 7), (0, 126)))
    boxes, spread = relay(owners, 0, (orbitals[0], padded))
    corners = spread[:, 0, :2]
    scalars = (owner.reshape(1), pairs, corners)

    planes = lax.dynamic_slice_in_dim(boxes, owner * depth, depth, 1).astype(jnp.float32)
    planes = planes.reshape(owners, depth, side, side)
    along_rows = placer(corners[:, 0], grid, side)
    along_cols = placer(corners[:, 1], grid, side)
    partial = jnp.einsum("izyx,ihx->izyh", planes * planes, along_cols, precision=PRECISE)
    partial = jnp.einsum("igy,izyh->zgh", along_rows, partial, precision=PRECISE)
    partial = partial.reshape(depth, grid * grid)
    density = partial
    for step in range(1, groups):
        density = density + lax.ppermute(partial, "grp", [(g, (g + step) % groups) for g in range(groups)])

    each = pairs.shape[0] // owners
    rho = local_call(
        functools.partial(pair_kernel, each, side), (each, levels, cells), scalars, (boxes,), "pair_density"
    )
    green = green_table(levels, side) * (1.0 / float(8 * levels * cells))
    along_z = cas_table(2 * levels, levels)
    along_y = cas_table(2 * side, side)
    fields = []
    for turn in range(each):
        value = rotate("kz,zc->kc", along_z, rho[turn]).reshape(2 * levels, side, side)
        value = rotate("ky,zyx->zkx", along_y, value)
        value = rotate("kx,zyx->zyk", along_y, value)
        value = value * green
        value = rotate("kx,zyk->zyx", along_y, value)
        value = rotate("ky,zkx->zyx", along_y, value).reshape(2 * levels, cells)
        fields.append(rotate("kz,kc->zc", along_z, value))
    field = jnp.concatenate(fields) if each > 1 else fields[0]

    external = lax.dynamic_slice_in_dim(ext_pot, owner * depth, depth, 0)
    potential = external.astype(jnp.float32) - EXCHANGE_COEF * jnp.cbrt(density)
    potential = potential.reshape(depth, grid, grid)
    read = jnp.einsum("igy,zgh->izyh", along_rows, potential, precision=PRECISE)
    read = jnp.einsum("izyh,ihx->izyx", read, along_cols, precision=PRECISE)
    read = read.reshape(owners, depth, cells)
    every, landed = relay(owners, 1, (field,), (read,))
    every = every.reshape(owners * each, levels, cells)
    gradient = local_call(
        functools.partial(combine_kernel, side),
        (levels, cells),
        scalars,
        (boxes, every, landed, orbitals[0]),
        "combine",
    )
    return gradient[None]


def solution(mesh):
    in_specs = (P(("grp", "own"), None, None), P(("grp", "own"), None), P("grp", None), P())
    out_specs = P(("grp", "own"), None, None)
    run = functools.partial(body, mesh.shape["own"], mesh.shape["grp"])
    return jax.shard_map(run, mesh=mesh, in_specs=in_specs, out_specs=out_specs, check_vma=False)
```

```python
import functools
import math

import jax
import jax.numpy as jnp
from jax import lax
from jax.experimental import pallas as pl
from jax.experimental.pallas import tpu as pltpu
from jax.sharding import PartitionSpec as P

SCREEN = 0.0025
MIXING = 0.25
EXCHANGE_COEF = (3.0 / math.pi) ** (1.0 / 3.0)
PRECISE = lax.Precision.HIGHEST
SPLIT = lax.Precision.HIGH
VMEM = pltpu.VMEM


def side_of(cells):
    return math.isqrt(cells)


def cas_table(length, count):
    row = lax.broadcasted_iota(jnp.int32, (length, count), 0)
    col = lax.broadcasted_iota(jnp.int32, (length, count), 1)
    angle = 2.0 * math.pi / length * (row * col % length).astype(jnp.float32)
    return jnp.cos(angle) + jnp.sin(angle)


def wave_squares(length):
    positions = jnp.arange(length, dtype=jnp.int32)
    signed = jnp.where(positions < length // 2, positions, positions - length)
    wavenumber = 2.0 * math.pi / length * signed.astype(jnp.float32)
    return wavenumber * wavenumber


def green_table(depth, width):
    along_z = wave_squares(2 * depth)
    along_y = wave_squares(2 * width)
    squared_sum = along_z[:, None, None] + along_y[None, :, None] + along_y[None, None, :]
    return 4.0 * math.pi / (squared_sum + SCREEN)


def rotate(pattern, matrix, operand):
    return jnp.einsum(pattern, matrix, operand, precision=SPLIT, preferred_element_type=jnp.float32)


def placer(starts, row_count, side):
    grid_index = lax.broadcasted_iota(jnp.int32, (starts.shape[0], row_count, side), 1)
    cell_index = lax.broadcasted_iota(jnp.int32, (starts.shape[0], row_count, side), 2)
    return (grid_index == cell_index + starts[:, None, None]).astype(jnp.float32)


def plane_split(count):
    rows = 1 << ((count.bit_length() - 1) // 2)
    return count // rows, rows


def relay_kernel(count, pieces, exchanged, *refs):
    far, near = plane_split(count)
    sources, slabs = refs[:pieces], refs[pieces : pieces + exchanged]
    refs = refs[pieces + exchanged :]
    targets, landings = refs[:pieces], refs[pieces : pieces + exchanged]
    send_sem, recv_sem, local_sem, slab_send, slab_recv = refs[pieces + exchanged :]
    me = lax.axis_index("own")
    z = me // near
    y = lax.rem(me, near)
    barrier = pltpu.get_barrier_semaphore()

    def across(step):
        return z * near + lax.rem(y + step, near)

    def signal(peer):
        pl.semaphore_signal(barrier, inc=1, device_id={"own": peer}, device_id_type=pl.DeviceIdType.MESH)

    if exchanged:
        for step in range(1, count):
            signal(lax.rem(me + step, count))
        pl.semaphore_wait(barrier, count - 1)
    else:
        for step in range(1, near):
            signal(across(step))
        pl.when(z > 0)(lambda: signal(me - near))
        pl.when(z < far - 1)(lambda: signal(me + near))
        pl.semaphore_wait(barrier, near - 1 + (z > 0).astype(jnp.int32) + (z < far - 1).astype(jnp.int32))

    parts = []
    for piece, source in enumerate(sources):
        rows = source.shape[0]
        if piece == 0:
            front = rows // 2 if source.dtype == jnp.bfloat16 else rows // 4
            parts.append((piece, 0, front, False))
            parts.append((piece, front, rows - front, True))
        else:
            parts.append((piece, 0, rows, True))
    fronts = [i for i, part in enumerate(parts) if not part[3]]
    backs = [i for i, part in enumerate(parts) if part[3]]

    def copy(index, origin, lane, peer, own):
        piece, start, size, _ = parts[index]
        rows = pl.ds(start, size)
        source = sources[piece].at[rows] if own else targets[piece].at[origin, rows]
        return pltpu.make_async_remote_copy(
            src_ref=source,
            dst_ref=targets[piece].at[origin, rows],
            send_sem=send_sem.at[index, origin, lane],
            recv_sem=recv_sem.at[index, origin],
            device_id={"own": peer},
            device_id_type=pl.DeviceIdType.MESH,
        )

    def slab_copy(index, step):
        peer = lax.rem(me + step, count)
        return pltpu.make_async_remote_copy(
            src_ref=slabs[index].at[peer],
            dst_ref=landings[index].at[me],
            send_sem=slab_send.at[index, step],
            recv_sem=slab_recv.at[index, step],
            device_id={"own": peer},
            device_id_type=pl.DeviceIdType.MESH,
        )

    def both(index, origin, own, act):
        pl.when(z < far - 1)(lambda: act(copy(index, origin, 0, me + near, own)))
        pl.when(z > 0)(lambda: act(copy(index, origin, 1, me - near, own)))

    def sideways(index, origin, own, act):
        for step in range(1, near):
            act(copy(index, origin, 1 + step, across(step), own))

    def start(item):
        item.start()

    def sent(item):
        item.wait_send()

    def arrived(index, origin):
        copy(index, origin, 0, me, False).wait_recv()

    for index in backs:
        both(index, me, True, start)
    for index in fronts:
        sideways(index, me, True, start)
    for index in backs:
        sideways(index, me, True, start)
    for index in range(exchanged):
        for step in range(1, count):
            slab_copy(index, step).start()
    for index in fronts:
        both(index, me, True, start)
    locals_ = [
        pltpu.make_async_copy(sources[piece], targets[piece].at[me], local_sem.at[piece]) for piece in range(pieces)
    ]
    for index in range(exchanged):
        locals_.append(pltpu.make_async_copy(slabs[index].at[me], landings[index].at[me], local_sem.at[pieces + index]))
    for item in locals_:
        item.start()
    for step in range(1, near):
        for index in fronts:
            arrived(index, across(step))
            both(index, across(step), False, start)

    def hop(distance, direction):
        here = z - direction * distance
        inside = (here >= 0) & (here < far)
        onward = inside & (z + direction >= 0) & (z + direction < far)
        lane = 0 if direction > 0 else 1
        neighbour = me + direction * near
        return here, inside, onward, lane, neighbour

    def travel(act, receive):
        for distance in range(1, far):
            for direction in (1, -1):
                here, inside, onward, lane, neighbour = hop(distance, direction)
                for index in backs:
                    origin = here * near + y
                    if receive:
                        pl.when(inside)(functools.partial(arrived, index, origin))
                    pl.when(onward)(lambda: act(copy(index, origin, lane, neighbour, False)))
                    pl.when(inside)(lambda: sideways(index, origin, False, act))
                for index in fronts:
                    for step in range(near):
                        origin = here * near + lax.rem(y + step, near)
                        if receive:
                            pl.when(inside)(functools.partial(arrived, index, origin))
                        pl.when(onward)(lambda: act(copy(index, origin, lane, neighbour, False)))

    travel(start, True)
    for level in range(far):
        for step in range(1, near):
            for index in backs:
                arrived(index, level * near + lax.rem(y + step, near))
    for index in range(exchanged):
        for step in range(1, count):
            slab_copy(index, step).wait()
    for index in backs + fronts:
        both(index, me, True, sent)
        sideways(index, me, True, sent)
    for step in range(1, near):
        for index in fronts:
            both(index, across(step), False, sent)
    travel(sent, False)
    for item in locals_:
        item.wait()


def relay(count, collective_id, arrays, slabs=()):
    pieces, exchanged = len(arrays), len(slabs)
    _, near = plane_split(count)
    shapes = [jax.ShapeDtypeStruct((count,) + a.shape, a.dtype) for a in arrays]
    shapes += [jax.ShapeDtypeStruct(a.shape, a.dtype) for a in slabs]
    return pl.pallas_call(
        functools.partial(relay_kernel, count, pieces, exchanged),
        out_shape=shapes,
        in_specs=[pl.BlockSpec(memory_space=VMEM)] * (pieces + exchanged),
        out_specs=[pl.BlockSpec(memory_space=VMEM)] * (pieces + exchanged),
        scratch_shapes=[
            pltpu.SemaphoreType.DMA((pieces + 1, count, near + 1)),
            pltpu.SemaphoreType.DMA((pieces + 1, count)),
            pltpu.SemaphoreType.DMA((pieces + exchanged,)),
            pltpu.SemaphoreType.DMA((max(exchanged, 1), count)),
            pltpu.SemaphoreType.DMA((max(exchanged, 1), count)),
        ],
        compiler_params=pltpu.CompilerParams(collective_id=collective_id, has_side_effects=True),
        name="relay",
    )(*arrays, *slabs)


def slide(value, shift_y, shift_x, side):
    cells = value.shape[1]
    lane = lax.broadcasted_iota(jnp.int32, value.shape, 1)
    y = lane // side - shift_y
    x = lax.rem(lane, side) - shift_x
    inside = (y >= 0) & (y < side) & (x >= 0) & (x < side)
    amount = lax.rem(shift_y * side + shift_x + 2 * cells, cells)
    return jnp.where(inside, pltpu.roll(value, amount, axis=1), 0.0)


def pair_kernel(each, side, owner_ref, pairs, corners, boxes, rho):
    base = owner_ref[0] * each
    for turn in range(each):
        first, second = pairs[base + turn, 0], pairs[base + turn, 1]
        dy = corners[second, 0] - corners[first, 0]
        dx = corners[second, 1] - corners[first, 1]
        moved = slide(boxes[second].astype(jnp.float32), dy, dx, side)
        rho[turn] = boxes[first].astype(jnp.float32) * moved


def combine_kernel(side, owner_ref, pairs, corners, boxes, fields, read, phi, out):
    me = owner_ref[0]
    owners, depth, _ = read.shape
    own = phi[...].astype(jnp.float32)
    for owner in range(owners):
        rows = slice(owner * depth, (owner + 1) * depth)
        out[rows, :] = read[owner] * own[rows, :]

    def step(row, carry):
        first, second = pairs[row, 0], pairs[row, 1]
        dy = corners[second, 0] - corners[first, 0]
        dx = corners[second, 1] - corners[first, 1]

        @pl.when(first == me)
        def _():
            moved = slide(boxes[second].astype(jnp.float32), dy, dx, side)
            out[...] -= MIXING * fields[row] * moved

        @pl.when(second == me)
        def _():
            product = fields[row] * boxes[first].astype(jnp.float32)
            out[...] -= MIXING * slide(product, -dy, -dx, side)

        return carry

    lax.fori_loop(0, pairs.shape[0], step, 0)


def local_call(kernel, shape, scalars, arrays, name):
    return pl.pallas_call(
        kernel,
        out_shape=jax.ShapeDtypeStruct(shape, jnp.float32),
        in_specs=[pl.BlockSpec(memory_space=pltpu.SMEM)] * len(scalars)
        + [pl.BlockSpec(memory_space=VMEM)] * len(arrays),
        out_specs=pl.BlockSpec(memory_space=VMEM),
        name=name,
    )(*scalars, *arrays)


def body(owners, groups, orbitals, offsets, pairs, ext_pot):
    owner = lax.axis_index("own")
    _, levels, cells = orbitals.shape
    side = side_of(cells)
    grid = side_of(ext_pot.shape[1])
    depth = levels // owners
    padded = jnp.pad(offsets, ((0, 7), (0, 126)))
    boxes, spread = relay(owners, 0, (orbitals[0], padded))
    corners = spread[:, 0, :2]
    scalars = (owner.reshape(1), pairs, corners)

    planes = lax.dynamic_slice_in_dim(boxes, owner * depth, depth, 1).astype(jnp.float32)
    planes = planes.reshape(owners, depth, side, side)
    along_rows = placer(corners[:, 0], grid, side)
    along_cols = placer(corners[:, 1], grid, side)
    partial = jnp.einsum("izyx,ihx->izyh", planes * planes, along_cols, precision=PRECISE)
    partial = jnp.einsum("igy,izyh->zgh", along_rows, partial, precision=PRECISE)
    partial = partial.reshape(depth, grid * grid)
    density = partial
    for step in range(1, groups):
        density = density + lax.ppermute(partial, "grp", [(g, (g + step) % groups) for g in range(groups)])

    each = pairs.shape[0] // owners
    rho = local_call(
        functools.partial(pair_kernel, each, side), (each, levels, cells), scalars, (boxes,), "pair_density"
    )
    green = green_table(levels, side) * (1.0 / float(8 * levels * cells))
    along_z = cas_table(2 * levels, levels)
    along_y = cas_table(2 * side, side)
    fields = []
    for turn in range(each):
        value = rotate("kz,zc->kc", along_z, rho[turn]).reshape(2 * levels, side, side)
        value = rotate("ky,zyx->zkx", along_y, value)
        value = rotate("kx,zyx->zyk", along_y, value)
        value = lax.optimization_barrier(value * green)
        value = rotate("kx,zyk->zyx", along_y, value)
        value = rotate("ky,zkx->zyx", along_y, value).reshape(2 * levels, cells)
        fields.append(rotate("kz,kc->zc", along_z, value))
    field = jnp.concatenate(fields) if each > 1 else fields[0]

    external = lax.dynamic_slice_in_dim(ext_pot, owner * depth, depth, 0)
    potential = external.astype(jnp.float32) - EXCHANGE_COEF * jnp.cbrt(density)
    potential = potential.reshape(depth, grid, grid)
    read = jnp.einsum("igy,zgh->izyh", along_rows, potential, precision=PRECISE)
    read = jnp.einsum("izyh,ihx->izyx", read, along_cols, precision=PRECISE)
    read = read.reshape(owners, depth, cells)
    every, landed = relay(owners, 1, (field,), (read,))
    every = every.reshape(owners * each, levels, cells)
    gradient = local_call(
        functools.partial(combine_kernel, side),
        (levels, cells),
        scalars,
        (boxes, every, landed, orbitals[0]),
        "combine",
    )
    return gradient[None]


def solution(mesh):
    in_specs = (P(("grp", "own"), None, None), P(("grp", "own"), None), P("grp", None), P())
    out_specs = P(("grp", "own"), None, None)
    run = functools.partial(body, mesh.shape["own"], mesh.shape["grp"])
    return jax.shard_map(run, mesh=mesh, in_specs=in_specs, out_specs=out_specs, check_vma=False)
```

```python
import functools
import math

import jax
import jax.numpy as jnp
from jax import lax
from jax.experimental import pallas as pl
from jax.experimental.pallas import tpu as pltpu
from jax.sharding import PartitionSpec as P

SCREEN = 0.0025
MIXING = 0.25
EXCHANGE_COEF = (3.0 / math.pi) ** (1.0 / 3.0)
PRECISE = lax.Precision.HIGHEST
SPLIT = lax.Precision.HIGH
VMEM = pltpu.VMEM


def side_of(cells):
    return math.isqrt(cells)


def cas_table(length, count):
    row = lax.broadcasted_iota(jnp.int32, (length, count), 0)
    col = lax.broadcasted_iota(jnp.int32, (length, count), 1)
    angle = 2.0 * math.pi / length * (row * col % length).astype(jnp.float32)
    return jnp.cos(angle) + jnp.sin(angle)


def wave_squares(length):
    positions = jnp.arange(length, dtype=jnp.int32)
    signed = jnp.where(positions < length // 2, positions, positions - length)
    wavenumber = 2.0 * math.pi / length * signed.astype(jnp.float32)
    return wavenumber * wavenumber


def green_table(depth, width):
    along_z = wave_squares(2 * depth)
    along_y = wave_squares(2 * width)
    squared_sum = along_z[:, None, None] + along_y[None, :, None] + along_y[None, None, :]
    return 4.0 * math.pi / (squared_sum + SCREEN)


def rotate(pattern, matrix, operand):
    return jnp.einsum(pattern, matrix, operand, precision=SPLIT, preferred_element_type=jnp.float32)


def placer(starts, row_count, side):
    grid_index = lax.broadcasted_iota(jnp.int32, (starts.shape[0], row_count, side), 1)
    cell_index = lax.broadcasted_iota(jnp.int32, (starts.shape[0], row_count, side), 2)
    return (grid_index == cell_index + starts[:, None, None]).astype(jnp.float32)


def plane_split(count):
    rows = 1 << ((count.bit_length() - 1) // 2)
    return count // rows, rows


def chunk_rows(array):
    rows = array.shape[0]
    if rows <= 8:
        return rows
    return rows // 2 if array.dtype == jnp.bfloat16 else rows // 4


def relay_kernel(count, pieces, exchanged, *refs):
    far, near = plane_split(count)
    sources, slabs = refs[:pieces], refs[pieces : pieces + exchanged]
    refs = refs[pieces + exchanged :]
    targets, landings = refs[:pieces], refs[pieces : pieces + exchanged]
    send_sem, recv_sem, local_sem, slab_send, slab_recv = refs[pieces + exchanged :]
    me = lax.axis_index("own")
    z = me // near
    y = lax.rem(me, near)
    barrier = pltpu.get_barrier_semaphore()

    def across(step):
        return z * near + lax.rem(y + step, near)

    def signal(peer):
        pl.semaphore_signal(barrier, inc=1, device_id={"own": peer}, device_id_type=pl.DeviceIdType.MESH)

    if exchanged:
        for step in range(1, count):
            signal(lax.rem(me + step, count))
        pl.semaphore_wait(barrier, count - 1)
    else:
        for step in range(1, near):
            signal(across(step))
        pl.when(z > 0)(lambda: signal(me - near))
        pl.when(z < far - 1)(lambda: signal(me + near))
        pl.semaphore_wait(barrier, near - 1 + (z > 0).astype(jnp.int32) + (z < far - 1).astype(jnp.int32))

    parts = []
    for piece, source in enumerate(sources):
        rows = source.shape[0]
        size = chunk_rows(source)
        for start_row in range(0, rows, size):
            parts.append((piece, start_row, size, piece > 0 or start_row > 0))
    fronts = [i for i, part in enumerate(parts) if not part[3]]
    backs = [i for i, part in enumerate(parts) if part[3]]

    def copy(index, origin, lane, peer, own):
        piece, start, size, _ = parts[index]
        rows = pl.ds(start, size)
        source = sources[piece].at[rows] if own else targets[piece].at[origin, rows]
        return pltpu.make_async_remote_copy(
            src_ref=source,
            dst_ref=targets[piece].at[origin, rows],
            send_sem=send_sem.at[index, origin, lane],
            recv_sem=recv_sem.at[index, origin],
            device_id={"own": peer},
            device_id_type=pl.DeviceIdType.MESH,
        )

    def slab_copy(index, step):
        peer = lax.rem(me + step, count)
        return pltpu.make_async_remote_copy(
            src_ref=slabs[index].at[peer],
            dst_ref=landings[index].at[me],
            send_sem=slab_send.at[index, step],
            recv_sem=slab_recv.at[index, step],
            device_id={"own": peer},
            device_id_type=pl.DeviceIdType.MESH,
        )

    def both(index, origin, own, act):
        pl.when(z < far - 1)(lambda: act(copy(index, origin, 0, me + near, own)))
        pl.when(z > 0)(lambda: act(copy(index, origin, 1, me - near, own)))

    def sideways(index, origin, own, act):
        for step in range(1, near):
            act(copy(index, origin, 1 + step, across(step), own))

    def start(item):
        item.start()

    def sent(item):
        item.wait_send()

    def arrived(index, origin):
        copy(index, origin, 0, me, False).wait_recv()

    for index in backs:
        both(index, me, True, start)
    for index in fronts:
        sideways(index, me, True, start)
    for index in backs:
        sideways(index, me, True, start)
    for index in fronts:
        both(index, me, True, start)
    for index in range(exchanged):
        for step in range(1, count):
            slab_copy(index, step).start()
    locals_ = [
        pltpu.make_async_copy(sources[piece], targets[piece].at[me], local_sem.at[piece]) for piece in range(pieces)
    ]
    for index in range(exchanged):
        locals_.append(pltpu.make_async_copy(slabs[index].at[me], landings[index].at[me], local_sem.at[pieces + index]))
    for item in locals_:
        item.start()
    for step in range(1, near):
        for index in fronts:
            arrived(index, across(step))
            both(index, across(step), False, start)

    def hop(distance, direction):
        here = z - direction * distance
        inside = (here >= 0) & (here < far)
        onward = inside & (z + direction >= 0) & (z + direction < far)
        lane = 0 if direction > 0 else 1
        neighbour = me + direction * near
        return here, inside, onward, lane, neighbour

    def travel(act, receive):
        for distance in range(1, far):
            for direction in (1, -1):
                here, inside, onward, lane, neighbour = hop(distance, direction)
                for index in backs:
                    origin = here * near + y
                    if receive:
                        pl.when(inside)(functools.partial(arrived, index, origin))
                    pl.when(onward)(lambda: act(copy(index, origin, lane, neighbour, False)))
                    pl.when(inside)(lambda: sideways(index, origin, False, act))
                for index in fronts:
                    for step in range(near):
                        origin = here * near + lax.rem(y + step, near)
                        if receive:
                            pl.when(inside)(functools.partial(arrived, index, origin))
                        pl.when(onward)(lambda: act(copy(index, origin, lane, neighbour, False)))

    travel(start, True)
    for level in range(far):
        for step in range(1, near):
            for index in backs:
                arrived(index, level * near + lax.rem(y + step, near))
    for index in range(exchanged):
        for step in range(1, count):
            slab_copy(index, step).wait()
    for index in backs + fronts:
        both(index, me, True, sent)
        sideways(index, me, True, sent)
    for step in range(1, near):
        for index in fronts:
            both(index, across(step), False, sent)
    travel(sent, False)
    for item in locals_:
        item.wait()


def relay(count, collective_id, arrays, slabs=()):
    pieces, exchanged = len(arrays), len(slabs)
    parts = sum(a.shape[0] // chunk_rows(a) for a in arrays)
    _, near = plane_split(count)
    shapes = [jax.ShapeDtypeStruct((count,) + a.shape, a.dtype) for a in arrays]
    shapes += [jax.ShapeDtypeStruct(a.shape, a.dtype) for a in slabs]
    return pl.pallas_call(
        functools.partial(relay_kernel, count, pieces, exchanged),
        out_shape=shapes,
        in_specs=[pl.BlockSpec(memory_space=VMEM)] * (pieces + exchanged),
        out_specs=[pl.BlockSpec(memory_space=VMEM)] * (pieces + exchanged),
        scratch_shapes=[
            pltpu.SemaphoreType.DMA((parts, count, near + 1)),
            pltpu.SemaphoreType.DMA((parts, count)),
            pltpu.SemaphoreType.DMA((pieces + exchanged,)),
            pltpu.SemaphoreType.DMA((max(exchanged, 1), count)),
            pltpu.SemaphoreType.DMA((max(exchanged, 1), count)),
        ],
        compiler_params=pltpu.CompilerParams(collective_id=collective_id, has_side_effects=True),
        name="relay",
    )(*arrays, *slabs)


def slide(value, shift_y, shift_x, side):
    cells = value.shape[1]
    lane = lax.broadcasted_iota(jnp.int32, value.shape, 1)
    y = lane // side - shift_y
    x = lax.rem(lane, side) - shift_x
    inside = (y >= 0) & (y < side) & (x >= 0) & (x < side)
    amount = lax.rem(shift_y * side + shift_x + 2 * cells, cells)
    return jnp.where(inside, pltpu.roll(value, amount, axis=1), 0.0)


def pair_kernel(each, side, owner_ref, pairs, corners, boxes, rho):
    base = owner_ref[0] * each
    for turn in range(each):
        first, second = pairs[base + turn, 0], pairs[base + turn, 1]
        dy = corners[second, 0] - corners[first, 0]
        dx = corners[second, 1] - corners[first, 1]
        moved = slide(boxes[second].astype(jnp.float32), dy, dx, side)
        rho[turn] = boxes[first].astype(jnp.float32) * moved


def combine_kernel(side, owner_ref, pairs, corners, boxes, fields, read, phi, out):
    me = owner_ref[0]
    owners, depth, _ = read.shape
    own = phi[...].astype(jnp.float32)
    for owner in range(owners):
        rows = slice(owner * depth, (owner + 1) * depth)
        out[rows, :] = read[owner] * own[rows, :]

    def step(row, carry):
        first, second = pairs[row, 0], pairs[row, 1]
        dy = corners[second, 0] - corners[first, 0]
        dx = corners[second, 1] - corners[first, 1]

        @pl.when(first == me)
        def _():
            moved = slide(boxes[second].astype(jnp.float32), dy, dx, side)
            out[...] -= MIXING * fields[row] * moved

        @pl.when(second == me)
        def _():
            product = fields[row] * boxes[first].astype(jnp.float32)
            out[...] -= MIXING * slide(product, -dy, -dx, side)

        return carry

    lax.fori_loop(0, pairs.shape[0], step, 0)


def local_call(kernel, shape, scalars, arrays, name):
    return pl.pallas_call(
        kernel,
        out_shape=jax.ShapeDtypeStruct(shape, jnp.float32),
        in_specs=[pl.BlockSpec(memory_space=pltpu.SMEM)] * len(scalars)
        + [pl.BlockSpec(memory_space=VMEM)] * len(arrays),
        out_specs=pl.BlockSpec(memory_space=VMEM),
        name=name,
    )(*scalars, *arrays)


def body(owners, groups, orbitals, offsets, pairs, ext_pot):
    owner = lax.axis_index("own")
    _, levels, cells = orbitals.shape
    side = side_of(cells)
    grid = side_of(ext_pot.shape[1])
    depth = levels // owners
    padded = jnp.pad(offsets, ((0, 7), (0, 126)))
    boxes, spread = relay(owners, 0, (orbitals[0], padded))
    corners = spread[:, 0, :2]
    scalars = (owner.reshape(1), pairs, corners)

    planes = lax.dynamic_slice_in_dim(boxes, owner * depth, depth, 1).astype(jnp.float32)
    planes = planes.reshape(owners, depth, side, side)
    along_rows = placer(corners[:, 0], grid, side)
    along_cols = placer(corners[:, 1], grid, side)
    partial = jnp.einsum("izyx,ihx->izyh", planes * planes, along_cols, precision=PRECISE)
    partial = jnp.einsum("igy,izyh->zgh", along_rows, partial, precision=PRECISE)
    partial = partial.reshape(depth, grid * grid)
    density = partial
    for step in range(1, groups):
        density = density + lax.ppermute(partial, "grp", [(g, (g + step) % groups) for g in range(groups)])

    each = pairs.shape[0] // owners
    rho = local_call(
        functools.partial(pair_kernel, each, side), (each, levels, cells), scalars, (boxes,), "pair_density"
    )
    green = green_table(levels, side) * (1.0 / float(8 * levels * cells))
    along_z = cas_table(2 * levels, levels)
    along_y = cas_table(2 * side, side)
    fields = []
    for turn in range(each):
        value = rotate("kz,zc->kc", along_z, rho[turn]).reshape(2 * levels, side, side)
        value = rotate("ky,zyx->zkx", along_y, value)
        value = rotate("kx,zyx->zyk", along_y, value)
        value = lax.optimization_barrier(value * green)
        value = rotate("kx,zyk->zyx", along_y, value)
        value = rotate("ky,zkx->zyx", along_y, value).reshape(2 * levels, cells)
        fields.append(rotate("kz,kc->zc", along_z, value))
    field = jnp.concatenate(fields) if each > 1 else fields[0]

    external = lax.dynamic_slice_in_dim(ext_pot, owner * depth, depth, 0)
    potential = external.astype(jnp.float32) - EXCHANGE_COEF * jnp.cbrt(density)
    potential = potential.reshape(depth, grid, grid)
    read = jnp.einsum("igy,zgh->izyh", along_rows, potential, precision=PRECISE)
    read = jnp.einsum("izyh,ihx->izyx", read, along_cols, precision=PRECISE)
    read = read.reshape(owners, depth, cells)
    every, landed = relay(owners, 1, (field,), (read,))
    every = every.reshape(owners * each, levels, cells)
    gradient = local_call(
        functools.partial(combine_kernel, side),
        (levels, cells),
        scalars,
        (boxes, every, landed, orbitals[0]),
        "combine",
    )
    return gradient[None]


def solution(mesh):
    in_specs = (P(("grp", "own"), None, None), P(("grp", "own"), None), P("grp", None), P())
    out_specs = P(("grp", "own"), None, None)
    run = functools.partial(body, mesh.shape["own"], mesh.shape["grp"])
    return jax.shard_map(run, mesh=mesh, in_specs=in_specs, out_specs=out_specs, check_vma=False)
```
